32 devices in a mesh: grp: 2 (over core), seq: 8 (over z, y), fsdp: 2 (over x).
Axes of the slice: x: 2, y: 2, z: 4, core: 2. Of those that a mesh axis runs over, the one named last changes fastest.
Arguments:
- new_rows: bfloat16 [1024, 5120], P('seq'), may hold values from -6 to 6
- cache_keys: bfloat16 [4, 512, 3072], P(None, None, 'fsdp'), may hold values from -16 to 16
- cache_values: bfloat16 [4, 512, 3072], P(None, None, 'fsdp'), may hold values from -6 to 6
- cache_frames: int32 [3], replicated, may hold values from 0 to 3
- real_bank: bfloat16 [2, 1024, 5120], P(None, 'seq'), may hold values from -6 to 6
- real_pick: int32 [1024], P('seq'), may hold values from 0 to 1
- attn_weights: bfloat16 [2, 3, 5120, 3072], P('grp', None, 'seq', 'fsdp'), may hold values from -1 to 1
- out_weights: bfloat16 [2, 3072, 5120], P('grp', 'seq', 'fsdp'), may hold values from -0.109375 to 0.109375
- norm_gains: float32 [2, 5120], P('grp'), may hold values from 0.5 to 1.5
- head_in: bfloat16 [5120, 128], P('fsdp'), may hold values from -0.078125 to 0.078125
- head_out: float32 [128], replicated, may hold values from -0.5 to 0.5
Outputs:
- wo_grads: bfloat16 [2, 3072, 5120], P('grp', 'seq', 'fsdp')
- losses: bfloat16 [2], P('grp')
The draws below stay inside these ranges and needn't reach their ends.
All inputs are finite; a program needn't handle non-finite values.
Results may differ from the reference program's by a relative error of at most 0.014.
The reference program's roundings to bfloat16 on the way (of `gen_heads`, `generated`, `gen_cot`, `head_grad` and `input_grad`) count: a program that leaves them out, or rounds other values in their place, can miss the bound.
Values may be sent and summed in bfloat16 or wider, within the bound.
A program may use at most 192 MiB of HBM per device.

```python
import jax
import jax.numpy as jnp
from jax import lax

D = 5120
HEADS = 24
HD = 128
UNITS = 128
ROWS = 128
SINK = 1
WINDOW = 2
HIST = 4
BANK = 2
NEWTOK = 1024
FRAME = 512
N_SEQ = 8
N_FSDP = 2


def planted_columns(key):
    head_key = jax.random.fold_in(key, 9101)
    chosen = jax.random.randint(jax.random.fold_in(head_key, 1), (), 0, HEADS)
    sign_vector = jnp.where(jax.random.bernoulli(jax.random.fold_in(head_key, 2), 0.5, (HD,)), 1.0, -1.0)
    magnitude = jax.random.uniform(jax.random.fold_in(head_key, 3), (HD,), jnp.float32, 0.5, 1.5)
    direction = sign_vector * magnitude
    column_head = jnp.arange(HEADS * HD) // HD
    return jnp.where(column_head == chosen, jnp.tile(direction, HEADS), 0.0)


def strength_factor(strength):
    return (strength / (1.083 * HD ** 0.5)) ** 0.5


def draw_attn_weights(key, part):
    spread = planted_columns(key)
    base = jax.random.truncated_normal(jax.random.fold_in(key, 9201), -4.0, 4.0, (2, 3, D, HEADS * HD), jnp.float32) * D ** (-0.5)
    row_sign = jnp.where(jax.random.bernoulli(jax.random.fold_in(key, 9202), 0.5, (2, 1, D, 1)), 1.0, -1.0)
    row_size = jax.random.uniform(jax.random.fold_in(key, 9203), (2, 1, D, 1), jnp.float32, 0.5, 1.5)
    factor = strength_factor(40.0)
    member_mask = jnp.array([1.0, 1.0, 0.0], jnp.float32).reshape(1, 3, 1, 1)
    planted = factor * row_sign * row_size * D ** (-0.5) * member_mask * spread
    return jnp.clip(base + planted, -1.0, 1.0).astype(jnp.bfloat16)


def draw_cache_keys(key, part):
    spread = planted_columns(key)
    base = jax.random.truncated_normal(jax.random.fold_in(key, 9301), -6.0, 6.0, (HIST, FRAME, HEADS * HD), jnp.float32)
    token_size = jax.random.normal(jax.random.fold_in(key, 9302), (HIST, FRAME, 1), jnp.float32)
    factor = strength_factor(40.0)
    return jnp.clip(base + factor * token_size * spread, -16.0, 16.0).astype(jnp.bfloat16)


def plant(entries, own_key, low, top_value):
    dims = entries.shape
    index_at = [jax.random.randint(jax.random.fold_in(own_key, axis), (), 0, dims[axis]) for axis in range(len(dims))]
    entries = entries.at[tuple(index_at)].set(low)
    longest = dims.index(max(dims))
    index_at[longest] = (index_at[longest] + 1) % dims[longest]
    return entries.at[tuple(index_at)].set(top_value)


def levels(own_key, dims, cuts, low, top_value):
    def one(position, blocks):
        draws = jax.random.uniform(jax.random.fold_in(jax.random.fold_in(own_key, 6), position), (blocks,), jnp.float32, low / len(cuts), top_value / len(cuts))
        return jnp.repeat(jnp.exp(draws), dims[position] // blocks).reshape((-1,) + (1,) * (len(dims) - position - 1))

    factor_of = one(*cuts[0])
    for cut in cuts[1:]:
        factor_of = factor_of * one(*cut)
    return factor_of


def bell_draw(stream_key, extent, deviation, limit, cuts=(), kind=jnp.bfloat16):
    level = levels(stream_key, extent, cuts, -0.22, 0.18) if cuts else 1.0
    result = jax.random.normal(stream_key, extent, jnp.float32) * deviation * level
    return jnp.minimum(jnp.maximum(result, -limit), limit).astype(kind)


def setup_inputs(seed: int = 0) -> dict:
    streams_of = jax.random.split(jax.random.key(seed), 12)
    new_rows = bell_draw(streams_of[0], (NEWTOK, D), 1.0, 6.0, ((0, 8),))
    cache_keys = draw_cache_keys(jax.random.fold_in(streams_of[11], 71), 0)
    cache_values = bell_draw(streams_of[2], (HIST, FRAME, HEADS * HD), 1.0, 6.0, ((2, 2),))
    cache_frames = jax.random.randint(streams_of[3], (SINK + WINDOW,), 0, HIST).astype(jnp.int32)
    real_bank = bell_draw(streams_of[4], (BANK, NEWTOK, D), 1.0, 6.0, ((1, 8),))
    real_pick = plant(jax.random.randint(streams_of[5], (NEWTOK,), 0, BANK), jax.random.fold_in(streams_of[5], 1), 0, BANK - 1).astype(jnp.int32)
    attn_weights = draw_attn_weights(jax.random.fold_in(streams_of[11], 71), 0)
    out_weights = bell_draw(streams_of[7], (2, HEADS * HD, D), (HEADS * HD) ** -0.5, 0.109375, ((0, 2), (1, 8), (2, 2)))
    norm_gains = jnp.clip(1.0 + 0.1 * jax.random.normal(streams_of[8], (2, D), jnp.float32), 0.5, 1.5)
    head_in = bell_draw(streams_of[9], (D, UNITS), D ** -0.5, 0.078125, ((0, 2),))
    head_out = bell_draw(streams_of[10], (UNITS,), UNITS ** -0.5, 0.5, (), jnp.float32)
    return {"new_rows": new_rows, "cache_keys": cache_keys, "cache_values": cache_values, "cache_frames": cache_frames, "real_bank": real_bank, "real_pick": real_pick, "attn_weights": attn_weights, "out_weights": out_weights, "norm_gains": norm_gains, "head_in": head_in, "head_out": head_out}


EPS = 1e-06
NEG = -1e+30

def rounded(value):
    return lax.optimization_barrier(value.astype(jnp.bfloat16)).astype(jnp.float32)

def project(row_block, gain_vector, weight_set):
    lifted = row_block.astype(jnp.float32)
    inverse = lax.rsqrt(lax.optimization_barrier(jnp.mean(lifted * lifted, axis=-1, keepdims=True)) + EPS)
    normed = (lifted * inverse * gain_vector).astype(jnp.bfloat16)
    projected = [jnp.dot(normed, weight_set[member], preferred_element_type=jnp.float32).astype(jnp.bfloat16) for member in range(3)]
    return (lifted, inverse, projected)

def split_heads(matrix):
    return matrix.reshape(matrix.shape[0], HEADS, HD).transpose(1, 0, 2)

def merge_heads(stacked):
    return stacked.transpose(1, 0, 2).reshape(stacked.shape[1], HEADS * HD)

def softmax_rows(queries, key_set, allowed):
    scores = jnp.dot(queries, key_set.T, preferred_element_type=jnp.float32) * HD ** (-0.5)
    scores = jnp.where(allowed, scores, NEG)
    row_max = lax.optimization_barrier(jnp.max(scores, axis=-1, keepdims=True))
    raised = jnp.exp(scores - row_max)
    return raised / lax.optimization_barrier(jnp.sum(raised, axis=-1, keepdims=True))

def attention(queries, key_set, value_set, allowed):

    def one_head(inputs):
        weights = softmax_rows(inputs[0], inputs[1], allowed)
        return jnp.dot(weights.astype(jnp.bfloat16), inputs[2], preferred_element_type=jnp.float32)
    stacked = lax.map(one_head, (split_heads(queries), split_heads(key_set), split_heads(value_set)))
    return merge_heads(stacked).astype(jnp.bfloat16)

def unit_direction(unit_values, head_out, head_in):
    _, gelu_back = jax.vjp(jax.nn.gelu, unit_values)
    unit_grad = gelu_back(jnp.broadcast_to(head_out, unit_values.shape))[0].astype(jnp.bfloat16)
    return jnp.dot(unit_grad, head_in.T, preferred_element_type=jnp.float32)

def block_grads(pairs):
    width = pairs[0][0].shape[1]
    total = jnp.zeros((width, D), jnp.float32)

    def step(block_index, carried):
        first_row = (block_index * ROWS).astype(jnp.int32)
        term = jnp.zeros((width, D), jnp.float32)
        for lead_heads, cotangent in pairs:
            lead_block = lax.dynamic_slice_in_dim(lead_heads, first_row, ROWS, 0)
            cot_block = lax.dynamic_slice_in_dim(cotangent, first_row, ROWS, 0)
            term = term + jnp.dot(lead_block.T, cot_block, preferred_element_type=jnp.float32)
        return carried + rounded(term)
    return lax.fori_loop(0, N_SEQ, step, total).astype(jnp.bfloat16)

def pick_rows(real_bank, real_pick):
    chosen = jnp.zeros(real_bank.shape[1:], real_bank.dtype)
    for entry in range(real_bank.shape[0]):
        chosen = jnp.where((real_pick == entry)[:, None], real_bank[entry], chosen)
    return chosen

def reference(new_rows, cache_keys, cache_values, cache_frames, real_bank, real_pick, attn_weights, out_weights, norm_gains, head_in, head_out):
    frame_len = NEWTOK // 2
    scale = HD ** (-0.5)
    _, _, (gen_q, gen_k, gen_v) = project(new_rows, norm_gains[0], attn_weights[0])
    picked_keys = cache_keys[cache_frames].reshape(-1, HEADS * HD)
    picked_values = cache_values[cache_frames].reshape(-1, HEADS * HD)
    token_frame = jnp.arange(NEWTOK) // frame_len
    gen_allowed = jnp.concatenate([jnp.ones((NEWTOK, picked_keys.shape[0]), jnp.bool_), token_frame[None, :] <= token_frame[:, None]], axis=1)
    gen_heads = attention(gen_q, jnp.concatenate([picked_keys, gen_k], axis=0), jnp.concatenate([picked_values, gen_v], axis=0), gen_allowed)
    generated = (new_rows.astype(jnp.float32) + jnp.dot(gen_heads, out_weights[0], preferred_element_type=jnp.float32)).astype(jnp.bfloat16)
    full_mask = jnp.ones((NEWTOK, NEWTOK), jnp.bool_)

    def critic(clip_rows):
        lifted, inverse, (crit_q, crit_k, crit_v) = project(clip_rows, norm_gains[1], attn_weights[1])
        heads = attention(crit_q, crit_k, crit_v, full_mask)
        outputs = (lifted + jnp.dot(heads, out_weights[1], preferred_element_type=jnp.float32)).astype(jnp.bfloat16)
        unit_values = jnp.dot(outputs, head_in, preferred_element_type=jnp.float32)
        return (lifted, inverse, crit_q, crit_k, crit_v, heads, unit_values)
    real_rows = pick_rows(real_bank, real_pick)
    _, _, _, _, _, real_heads, real_units = critic(real_rows)
    fake_lifted, fake_inverse, fake_q, fake_k, fake_v, fake_heads, fake_units = critic(generated)
    real_score = jnp.sum(jax.nn.gelu(real_units) * head_out)
    fake_score = jnp.sum(jax.nn.gelu(fake_units) * head_out)
    margin = (real_score - fake_score) / NEWTOK
    losses = jnp.stack([jax.nn.softplus(margin), jax.nn.softplus(-margin)]).astype(jnp.bfloat16)
    real_dir = unit_direction(real_units, head_out, head_in)
    fake_dir = unit_direction(fake_units, head_out, head_in)
    real_cot = (-jax.nn.sigmoid(-margin) * real_dir).astype(jnp.bfloat16)
    fake_cot = (jax.nn.sigmoid(-margin) * fake_dir).astype(jnp.bfloat16)
    gen_cot = (-jax.nn.sigmoid(margin) * fake_dir).astype(jnp.bfloat16)
    col_count = D // N_FSDP
    head_sum = jnp.zeros((NEWTOK, HEADS * HD), jnp.float32)
    for group_index in range(N_FSDP):
        low = group_index * col_count
        term = jnp.dot(gen_cot[:, low:low + col_count], out_weights[1][:, low:low + col_count].T, preferred_element_type=jnp.float32)
        head_sum = head_sum + rounded(term)
    head_grad = head_sum.astype(jnp.bfloat16)

    def head_back(inputs):
        queries, key_set, value_set, grad_out = inputs
        weights = softmax_rows(queries, key_set, full_mask)
        slopes = jnp.dot(grad_out, value_set.T, preferred_element_type=jnp.float32)
        score_grad = (weights * (slopes - lax.optimization_barrier(jnp.sum(slopes * weights, axis=-1, keepdims=True)))).astype(jnp.bfloat16)
        query_grad = jnp.dot(score_grad, key_set, preferred_element_type=jnp.float32) * scale
        score_blocks = score_grad.astype(jnp.float32).reshape(N_SEQ, ROWS, NEWTOK)
        query_blocks = queries.astype(jnp.float32).reshape(N_SEQ, ROWS, HD)
        key_parts = jnp.einsum('srk,srd->skd', score_blocks, query_blocks) * scale
        key_grad = lax.optimization_barrier(jnp.sum(rounded(key_parts), axis=0))
        weight_blocks = weights.astype(jnp.bfloat16).astype(jnp.float32).reshape(N_SEQ, ROWS, NEWTOK)
        grad_blocks = grad_out.astype(jnp.float32).reshape(N_SEQ, ROWS, HD)
        value_grad = lax.optimization_barrier(jnp.sum(rounded(jnp.einsum('srk,srd->skd', weight_blocks, grad_blocks)), axis=0))
        return (query_grad, key_grad, value_grad)
    query_g, key_g, value_g = lax.map(head_back, (split_heads(fake_q), split_heads(fake_k), split_heads(fake_v), split_heads(head_grad)))
    grads = [merge_heads(query_g).astype(jnp.bfloat16), merge_heads(key_g).astype(jnp.bfloat16), merge_heads(value_g).astype(jnp.bfloat16)]
    heads_per = HEADS * HD // N_FSDP
    row_grad = jnp.zeros((NEWTOK, D), jnp.float32)
    for group_index in range(N_FSDP):
        low = group_index * heads_per
        term = jnp.zeros((NEWTOK, D), jnp.float32)
        for member in range(3):
            term = term + jnp.dot(grads[member][:, low:low + heads_per], attn_weights[1][member][:, low:low + heads_per].T, preferred_element_type=jnp.float32)
        row_grad = row_grad + rounded(term)
    lifted_grad = row_grad * norm_gains[1]
    input_grad = (fake_inverse * lifted_grad + gen_cot.astype(jnp.float32)).astype(jnp.bfloat16)
    gen_grad = block_grads([(gen_heads, input_grad)])
    crit_grad = block_grads([(real_heads, real_cot), (fake_heads, fake_cot)])
    return (jnp.stack([gen_grad, crit_grad]), losses)
```

```python
import functools

import jax
import jax.numpy as jnp
from jax import lax
from jax.experimental import pallas as pl
from jax.experimental.pallas import tpu as pltpu
from jax.sharding import PartitionSpec as P

HD = 128


EPS = 1e-06
NEG = -1e30


def passed_along(value, axis, steps):
    count = lax.axis_size(axis)
    leading, last = (max(0, -steps), min(count, count - steps))
    return lax.ppermute(value, axis, [(source, source + steps) for source in range(leading, last)])


def attend(queries, key_set, value_set, allowed):
    head_size = queries.shape[-1]
    scores = jnp.einsum(
        "rhd,khd->hrk", queries, key_set, preferred_element_type=jnp.float32
    ) * head_size ** (-0.5)
    if allowed is not None:
        scores = jnp.where(allowed[None], scores, NEG)
    row_max = jnp.max(scores, axis=-1, keepdims=True)
    raised = jnp.exp(scores - row_max)
    weights = raised / jnp.sum(raised, axis=-1, keepdims=True)
    result = jnp.einsum(
        "hrk,khd->rhd", weights.astype(jnp.bfloat16), value_set, preferred_element_type=jnp.float32
    )
    return (result, weights)


PIECES = 4


def ring_kernel(count, parts, total, held, send_sems, recv_sems):
    me = lax.axis_index("seq")
    place = (1 - me % 2) * (me // 2) + (me % 2) * (count - 1 - me // 2)

    def device_at(position):
        wrapped = (position + 2 * count) % count
        upper = wrapped // (count // 2)
        return (1 - upper) * 2 * wrapped + upper * (2 * (count - 1 - wrapped) + 1)

    right, left = device_at(place + 1), device_at(place - 1)
    barrier = pltpu.get_barrier_semaphore()
    for neighbour in (left, right):
        pl.semaphore_signal(
            barrier,
            inc=1,
            device_id={"seq": neighbour},
            device_id_type=pl.DeviceIdType.MESH,
        )
    pl.semaphore_wait(barrier, 2)
    rows = total.shape[0] // PIECES
    flying = []
    for step in range(count):
        for piece in range(PIECES):
            forward = piece % 2 == 0
            sign = 1 if forward else -1
            span = pl.ds(piece * rows, rows)
            chunk = device_at(place - sign * (step + 1))
            if step == 0:
                source = parts.at[chunk, span, :]
            else:
                flying[(step - 1) * PIECES + piece].wait_recv()
                own = parts[chunk, span, :].astype(jnp.float32)
                added = held[step - 1, span, :].astype(jnp.float32) + own
                if step == count - 1:
                    total[span, :] = added.astype(total.dtype)
                    continue
                held[step - 1, span, :] = added.astype(held.dtype)
                source = held.at[step - 1, span, :]
            copy = pltpu.make_async_remote_copy(
                src_ref=source,
                dst_ref=held.at[step, span, :],
                send_sem=send_sems.at[step, piece],
                recv_sem=recv_sems.at[step, piece],
                device_id={"seq": right if forward else left},
                device_id_type=pl.DeviceIdType.MESH,
            )
            copy.start()
            flying.append(copy)
    for copy in flying:
        copy.wait_send()


def ring_sum(parts, collective_id):
    count, rows, cols = parts.shape
    return pl.pallas_call(
        functools.partial(ring_kernel, count),
        out_shape=jax.ShapeDtypeStruct((rows, cols), parts.dtype),
        in_specs=[pl.BlockSpec(memory_space=pltpu.VMEM)],
        out_specs=pl.BlockSpec(memory_space=pltpu.VMEM),
        scratch_shapes=[
            pltpu.VMEM((count - 1, rows, cols), parts.dtype),
            pltpu.SemaphoreType.DMA((count - 1, PIECES)),
            pltpu.SemaphoreType.DMA((count - 1, PIECES)),
        ],
        compiler_params=pltpu.CompilerParams(
            collective_id=collective_id, has_side_effects=True, vmem_limit_bytes=60 * 2**20
        ),
    )(parts)


def normalise(row_block, gain_vector):
    lifted = row_block.astype(jnp.float32)
    inverse = lax.rsqrt(jnp.mean(lifted * lifted, axis=-1, keepdims=True) + EPS)
    return ((lifted * inverse * gain_vector).astype(jnp.bfloat16), inverse)


def project(normed, weight_set, deal, kinds, collective_id):
    columns = lax.all_to_all(normed, "seq", 1, 0, tiled=True)
    span = deal * HD
    projected = []
    for member, kind in enumerate(kinds):
        weights = weight_set[:, :, member * span : (member + 1) * span]
        parts = jnp.einsum("td,sdx->stx", columns, weights, preferred_element_type=jnp.float32)
        total = ring_sum(parts.astype(kind), collective_id + member).astype(jnp.bfloat16)
        projected.append(total.reshape(total.shape[0], deal, HD))
    return projected


def unit_gradient(unit_values, head_out):
    _, gelu_back = jax.vjp(jax.nn.gelu, unit_values)
    return gelu_back(jnp.broadcast_to(head_out, unit_values.shape))[0].astype(jnp.bfloat16)


def direction(unit_grad, head_cols):
    return jnp.einsum("tu,cu->tc", unit_grad, head_cols, preferred_element_type=jnp.float32)


def pick_rows(real_bank, real_pick):
    chosen = jnp.zeros(real_bank.shape[1:], real_bank.dtype)
    for entry in range(real_bank.shape[0]):
        chosen = jnp.where((real_pick == entry)[:, None], real_bank[entry], chosen)
    return chosen


def local(
    new_rows,
    cache_keys,
    cache_values,
    cache_frames,
    real_bank,
    real_pick,
    attn_weights,
    out_weights,
    norm_gains,
    head_in,
    head_out,
):
    is_gen = lax.axis_index("grp") == 0
    grp_at = lax.axis_index("grp")
    seq_at = lax.axis_index("seq")
    fsdp_at = lax.axis_index("fsdp")
    seq_n = lax.axis_size("seq")
    grp_n = lax.axis_size("grp")
    row_count, width = new_rows.shape
    token_count = row_count * seq_n
    frame_len = token_count // 2
    own_weights = attn_weights[0]
    own_out = out_weights[0]
    col_count = own_out.shape[1]
    depth = own_weights.shape[1]
    heads_width = own_weights.shape[2]
    head_count = heads_width // HD
    start_col = fsdp_at * col_count
    half = col_count // grp_n
    chunk_at = start_col + grp_at * half

    deal_one = -(-head_count // seq_n)
    deal_two = -(-head_count // (seq_n * grp_n))

    def dealt(count):
        return jnp.pad(own_weights, ((0, 0), (0, 0), (0, count * HD - heads_width)))

    weights_one = (
        dealt(deal_one * seq_n)
        .reshape(3, depth, seq_n, deal_one * HD)
        .transpose(2, 1, 0, 3)
        .reshape(seq_n, depth, 3 * deal_one * HD)
    )
    weights_pair = (
        dealt(deal_two * seq_n * grp_n)
        .reshape(3, depth, seq_n, grp_n, deal_two * HD)
        .transpose(3, 2, 1, 0, 4)
        .reshape(grp_n, seq_n, depth, 3 * deal_two * HD)
    )
    critic_share = passed_along((weights_pair[0], norm_gains[0]), "grp", -1)
    weights_two = jnp.where(is_gen, critic_share[0], weights_pair[1])
    critic_gain = jnp.where(is_gen, critic_share[1], norm_gains[0])

    unit_map = jnp.dot(own_out, head_in, preferred_element_type=jnp.float32)
    unit_map = lax.psum(jnp.where(is_gen, 0.0, unit_map), ("grp", "fsdp"))
    unit_map = lax.all_gather(unit_map, "seq", axis=0, tiled=True)
    unit_map = lax.dynamic_slice_in_dim(unit_map, fsdp_at * heads_width, heads_width, 0)

    def own_map(count, deal, place):
        padded = jnp.pad(unit_map, ((0, count * HD - heads_width), (0, 0)))
        return lax.dynamic_slice_in_dim(padded, place * deal * HD, deal * HD, 0)

    map_one = own_map(deal_one * seq_n, deal_one, seq_at)
    map_two = own_map(deal_two * seq_n * grp_n, deal_two, seq_at * grp_n + grp_at)

    def clip_units(rows, heads, rows_map):
        cols = lax.dynamic_slice_in_dim(rows, start_col, col_count, 1)
        direct = jnp.dot(cols, head_in, preferred_element_type=jnp.float32)
        direct = jnp.where(is_gen, 0.0, direct)
        units = jnp.dot(heads.astype(jnp.float32), rows_map, precision=lax.Precision.HIGHEST)
        spot = lax.dynamic_slice_in_dim(units, seq_at * row_count, row_count, 0)
        return lax.dynamic_update_slice_in_dim(units, spot + direct, seq_at * row_count, 0)

    def to_columns(heads, deal):
        own_tokens = lax.all_to_all(heads, "seq", 0, 1, tiled=True)[:, :heads_width]
        whole = lax.all_gather(own_tokens, "fsdp", axis=1, tiled=True)
        return lax.all_to_all(whole, "seq", 1, 0, tiled=True)

    real_rows = pick_rows(real_bank, real_pick)
    first_rows = jnp.where(is_gen, new_rows, real_rows)
    normed, _ = normalise(first_rows, norm_gains[0])
    query_one, keys_one, values_one = project(normed, weights_one, deal_one, (jnp.float32,) * 3, 1)

    def generator_attend(operand):
        first = jnp.minimum(seq_at * deal_one, head_count - deal_one) * HD

        def picked(cache):
            mine = lax.dynamic_slice_in_dim(cache, first, deal_one * HD, 2)
            return jnp.take(mine, cache_frames, axis=0).reshape(-1, deal_one, HD)

        picked_keys = picked(cache_keys)
        picked_values = picked(cache_values)
        token_frame = jnp.arange(token_count) // frame_len
        allowed = jnp.concatenate(
            [
                jnp.ones((token_count, picked_keys.shape[0]), jnp.bool_),
                token_frame[None, :] <= token_frame[:, None],
            ],
            axis=1,
        )
        all_keys = jnp.concatenate([picked_keys, keys_one], axis=0)
        all_values = jnp.concatenate([picked_values, values_one], axis=0)
        return attend(query_one, all_keys, all_values, allowed)[0].astype(jnp.bfloat16)

    def critic_attend(operand):
        return attend(query_one, keys_one, values_one, None)[0].astype(jnp.bfloat16)

    first_heads = lax.cond(is_gen, generator_attend, critic_attend, 0).reshape(
        token_count, deal_one * HD
    )
    first_cols = to_columns(first_heads, deal_one)
    part = jnp.dot(first_cols, own_out, preferred_element_type=jnp.float32)
    shared = passed_along(part[:, half:], "grp", 1)
    part = jnp.where(is_gen, part[:, :half], shared)
    summed = ring_sum(part.reshape(seq_n, row_count, half), 7)
    chunk = lax.dynamic_slice_in_dim(new_rows, chunk_at, half, 1).astype(jnp.float32)
    chunk = (chunk + summed).astype(jnp.bfloat16)
    generated = lax.all_gather(chunk, ("fsdp", "grp"), axis=1, tiled=True)

    real_units = clip_units(real_rows, first_heads, map_one)
    real_units = lax.psum(jnp.where(is_gen, 0.0, real_units), ("grp", "seq", "fsdp"))
    generated, real_units = lax.optimization_barrier((generated, real_units))

    normed, inverse = normalise(generated, critic_gain)
    query_two, keys_two, values_two = project(
        normed, weights_two, deal_two, (jnp.float32, jnp.float32, jnp.bfloat16), 4
    )
    second_result, second_weights = attend(query_two, keys_two, values_two, None)
    second_heads = second_result.astype(jnp.bfloat16).reshape(token_count, deal_two * HD)
    fake_units = clip_units(generated, second_heads, map_two)
    fake_units = lax.psum(fake_units, ("grp", "seq", "fsdp"))
    paired = lax.all_gather(second_heads, "grp", axis=1, tiled=True)
    second_cols = to_columns(paired, deal_two * grp_n)

    real_score = jnp.sum(jax.nn.gelu(real_units) * head_out)
    fake_score = jnp.sum(jax.nn.gelu(fake_units) * head_out)
    margin = (real_score - fake_score) / token_count
    losses = jnp.where(is_gen, jax.nn.softplus(margin), jax.nn.softplus(-margin))
    real_grad = unit_gradient(real_units, head_out)
    fake_grad = unit_gradient(fake_units, head_out)
    gen_scale = -jax.nn.sigmoid(margin)

    head_grad = (
        gen_scale
        * jnp.einsum(
            "tu,hu->th", fake_grad.astype(jnp.float32), map_two, precision=lax.Precision.HIGHEST
        )
    ).astype(jnp.bfloat16)
    head_grad = head_grad.reshape(token_count, deal_two, HD)
    scale = HD ** (-0.5)
    slopes = jnp.einsum("rhd,khd->hrk", head_grad, values_two, preferred_element_type=jnp.float32)
    centred = jnp.sum(slopes * second_weights, axis=-1, keepdims=True)
    score_grad = (second_weights * (slopes - centred)).astype(jnp.bfloat16)
    query_grad = (
        jnp.einsum("hrk,khd->rhd", score_grad, keys_two, preferred_element_type=jnp.float32) * scale
    )
    key_grad = (
        jnp.einsum("hrk,rhd->khd", score_grad, query_two, preferred_element_type=jnp.float32)
        * scale
    )
    value_grad = jnp.einsum(
        "hrk,rhd->khd",
        second_weights.astype(jnp.bfloat16),
        head_grad,
        preferred_element_type=jnp.float32,
    )
    stacked = jnp.stack([query_grad, key_grad, value_grad], axis=1).astype(jnp.bfloat16)
    stacked = lax.all_gather(
        stacked.reshape(token_count, 3 * deal_two * HD), "seq", axis=0, tiled=False
    )
    critic_scale = jax.nn.sigmoid(-margin)
    real_cot = (-critic_scale * direction(real_grad, head_in)).astype(jnp.bfloat16)
    fake_cot = (critic_scale * direction(fake_grad, head_in)).astype(jnp.bfloat16)
    stacked, second_cols, real_cot, fake_cot = lax.optimization_barrier(
        (stacked, second_cols, real_cot, fake_cot)
    )
    row_terms = jnp.einsum(
        "stx,sdx->td", stacked, weights_two, preferred_element_type=jnp.float32
    ).astype(jnp.bfloat16)
    row_terms = lax.all_to_all(row_terms, "seq", 0, 1, tiled=True)
    row_grad = lax.psum_scatter(
        row_terms, ("fsdp", "grp"), scatter_dimension=1, tiled=True
    ).astype(jnp.float32)
    gain_chunk = lax.dynamic_slice_in_dim(critic_gain, chunk_at, half, 0)
    head_chunk = lax.dynamic_slice_in_dim(head_in, grp_at * half, half, 0)
    own_grad = lax.dynamic_slice_in_dim(fake_grad, seq_at * row_count, row_count, 0)
    gen_cot = (gen_scale * direction(own_grad, head_chunk)).astype(jnp.bfloat16)
    input_grad = (inverse * (row_grad * gain_chunk) + gen_cot.astype(jnp.float32)).astype(
        jnp.bfloat16
    )
    input_grad = lax.all_gather(input_grad, "seq", axis=0, tiled=True)
    other_half = passed_along(input_grad, "grp", -1)
    input_grad = jnp.concatenate([input_grad, other_half], axis=1)

    def product(heads, cotangent):
        return jnp.einsum("th,tc->hc", heads, cotangent, preferred_element_type=jnp.float32)

    wo_grad = lax.cond(
        is_gen,
        lambda _: product(first_cols, input_grad).astype(jnp.bfloat16),
        lambda _: (product(first_cols, real_cot) + product(second_cols, fake_cot)).astype(
            jnp.bfloat16
        ),
        0,
    )
    return (wo_grad[None], losses.astype(jnp.bfloat16)[None])


def solution(mesh):
    placed = (
        P("seq", None),
        P(None, None, "fsdp"),
        P(None, None, "fsdp"),
        P(),
        P(None, "seq", None),
        P("seq"),
        P("grp", None, "seq", "fsdp"),
        P("grp", "seq", "fsdp"),
        P("grp", None),
        P("fsdp", None),
        P(),
    )
    return jax.shard_map(
        local,
        mesh=mesh,
        in_specs=placed,
        out_specs=(P("grp", "seq", "fsdp"), P("grp")),
        check_vma=False,
    )
```
